32 devices in a mesh: alpha: 4 (over y, core), beta: 8 (over z, x).
Axes of the slice: x: 2, y: 2, z: 4, core: 2. Of those that a mesh axis runs over, the one named last changes fastest.
Arguments:
- coeff: float32 [128, 1024], P('alpha', 'beta'), may hold values from -6 to 6
- integrals: float32 [528, 528], replicated, as said below
- beta_pairs: int32 [1024, 230], P('beta'), may hold values from 0 to 527, as said below
- beta_targets: int32 [1024, 230], P('beta'), may hold values from 0 to 1023
- beta_signs: int32 [1024, 230], P('beta'), may hold values from -1 to 1, as said below
- alpha_pairs: int32 [128, 230], P('alpha'), may hold values from 0 to 527, as said below
- alpha_targets: int32 [128, 230], P('alpha'), may hold values from 0 to 127
- alpha_signs: int32 [128, 230], P('alpha'), may hold values from -1 to 1, as said below
Outputs:
- sigma: float32 [128, 1024], P('alpha', 'beta')
The draws below stay inside these ranges and needn't reach their ends.
Inputs may be any that keep to these rules, and one draw needn't show every extreme that they name: The 230 pairs of one row of beta_pairs are distinct. `beta_signs`: each sign is -1 or 1. The 230 pairs of one row of alpha_pairs are distinct. `alpha_signs`: each sign is -1 or 1. `integrals`: symmetric.
All inputs are finite; a program needn't handle non-finite values.
Results may differ from the reference program's by a relative error of at most 0.0003.
Values sent between devices are 32-bit elements; how exact they have to be, the bound alone decides.
No kernel may reach another device: no remote copies, remote signals or barrier semaphores. Data moves between devices by JAX's collectives and lax.ppermute only.
A program may use at most 128 MiB of HBM per device.

```python
import jax
import jax.numpy as jnp
from jax import lax

PAIRS = 528
EXC = 230
B_DEV = 128
NA = 128
NB = 1024


def draw_integrals(key, part):
    base = jax.random.normal(key, (PAIRS, PAIRS), jnp.float32)
    return ((base + base.T) * (0.7071 / EXC)).astype(jnp.float32)


def distinct_pairs(key, rows):
    keys = jax.random.split(key, rows)
    return jax.vmap(lambda single: jax.random.permutation(single, PAIRS)[:EXC])(keys).astype(jnp.int32)


def draw_beta_pairs(key, part):
    return distinct_pairs(jax.random.fold_in(key, 11), NB)


def draw_alpha_pairs(key, part):
    return distinct_pairs(jax.random.fold_in(key, 13), NA)


def draw_beta_signs(key, part):
    return (2 * jax.random.randint(jax.random.fold_in(key, 17), (NB, EXC), 0, 2) - 1).astype(jnp.int32)


def draw_alpha_signs(key, part):
    return (2 * jax.random.randint(jax.random.fold_in(key, 19), (NA, EXC), 0, 2) - 1).astype(jnp.int32)


def plant(result, rng, smallest, largest):
    longest = result.shape.index(max(result.shape))
    spots = []
    for shift in (0, 1):
        where = [jax.random.randint(jax.random.fold_in(rng, axis), (), 0, length) for axis, length in enumerate(result.shape)]
        where[longest] = (where[longest] + shift) % result.shape[longest]
        spots.append(tuple(where))
    return result.at[spots[0]].set(smallest).at[spots[1]].set(largest)


def block_levels(key, dims, cuts, low, high):
    gain, own = 1.0, jax.random.fold_in(key, 6)
    for dim, parts in cuts:
        draws = jnp.exp(jax.random.uniform(jax.random.fold_in(own, dim), (parts,), jnp.float32, low / len(cuts), high / len(cuts)))
        gain = gain * jnp.repeat(draws, dims[dim] // parts).reshape([-1 if axis == dim else 1 for axis in range(len(dims))])
    return gain


def scatter_about(rng, dims, width, most, pieces=(), held_as=jnp.bfloat16):
    factor_of = block_levels(rng, dims, pieces, -0.22, 0.18) if pieces else 1.0
    values = jax.random.normal(rng, dims, jnp.float32) * width * factor_of
    return jnp.minimum(jnp.maximum(values, -most), most).astype(held_as)


def setup_inputs(seed: int = 0) -> dict:
    key_list = jax.random.split(jax.random.key(seed), 9)
    coeff = scatter_about(key_list[0], (NA, NB), 1.0, 6.0, ((0, 4), (1, 8)), jnp.float32)
    integrals = draw_integrals(jax.random.fold_in(key_list[8], 71), 0)
    beta_pairs = draw_beta_pairs(jax.random.fold_in(key_list[8], 71), 0)
    beta_targets = plant(jax.random.randint(key_list[3], (NB, EXC), 0, NB), jax.random.fold_in(key_list[3], 1), 0, NB - 1).astype(jnp.int32)
    beta_signs = draw_beta_signs(jax.random.fold_in(key_list[8], 71), 0)
    alpha_pairs = draw_alpha_pairs(jax.random.fold_in(key_list[8], 71), 0)
    alpha_targets = plant(jax.random.randint(key_list[6], (NA, EXC), 0, NA), jax.random.fold_in(key_list[6], 1), 0, NA - 1).astype(jnp.int32)
    alpha_signs = draw_alpha_signs(jax.random.fold_in(key_list[8], 71), 0)
    return dict(coeff=coeff, integrals=integrals, beta_pairs=beta_pairs, beta_targets=beta_targets, beta_signs=beta_signs, alpha_pairs=alpha_pairs, alpha_targets=alpha_targets, alpha_signs=alpha_signs)


def reference(coeff, integrals, beta_pairs, beta_targets, beta_signs, alpha_pairs, alpha_targets, alpha_signs):
    alpha_count = coeff.shape[0]
    block_count = NB // B_DEV
    row_ids = jnp.arange(alpha_count, dtype=jnp.int32)[:, None]
    col_ids = jnp.arange(B_DEV, dtype=jnp.int32)[:, None]
    flat_targets = alpha_targets.reshape(-1)
    alpha_weight = alpha_signs.astype(jnp.float32)[:, :, None]

    def one_block(index):
        start = (index * B_DEV).astype(jnp.int32)
        targets = lax.dynamic_slice_in_dim(beta_targets, start, B_DEV, 0)
        pairs = lax.dynamic_slice_in_dim(beta_pairs, start, B_DEV, 0)
        signs = lax.dynamic_slice_in_dim(beta_signs, start, B_DEV, 0).astype(jnp.float32)
        values = jnp.take(coeff, targets, axis=1) * signs[None]
        lifted = jnp.zeros((alpha_count, B_DEV, PAIRS), jnp.float32).at[:, col_ids, pairs].add(values)
        mixed = jnp.dot(lifted.reshape(-1, PAIRS), integrals, precision=lax.Precision.HIGHEST,
                        preferred_element_type=jnp.float32).reshape(alpha_count, B_DEV, PAIRS)
        picked = mixed[row_ids, :, alpha_pairs] * alpha_weight
        return jnp.zeros((alpha_count, B_DEV), jnp.float32).at[flat_targets].add(picked.reshape(-1, B_DEV))

    blocks = lax.map(one_block, jnp.arange(block_count, dtype=jnp.int32))
    return jnp.transpose(blocks, (1, 0, 2)).reshape(alpha_count, NB)
```

```python
import functools

import jax
import jax.numpy as jnp
from jax import lax
from jax.experimental import pallas as pl
from jax.experimental.pallas import tpu as pltpu
from jax.sharding import PartitionSpec as P

BF = jnp.bfloat16
F32 = jnp.float32
I32 = jnp.int32
NT = (((1,), (1,)), ((), ()))


def split(x):
    hi = x.astype(BF)
    return hi, (x - hi.astype(F32)).astype(BF)


def fold_kernel(rows,pairs_ref,tg_ref,sg_ref,v_ref,g_ref,vcat,wcat,rows_p,rows_t,rows_s):
    n_pairs=v_ref.shape[0]; na=g_ref.shape[2]//2
    main=n_pairs//128*128; rest=n_pairs-main
    exc=pairs_ref.shape[1]; ew=rows_p.shape[0]*128
    @pl.when(pl.program_id(0)==0)
    def _():
        hi,lo=split(v_ref[...])
        vcat[:,:main]=hi[:,:main]; vcat[:,main:2*main]=lo[:,:main]
        vcat[:,2*main:2*main+rest]=hi[:,main:]; vcat[:,2*main+rest:2*main+2*rest]=lo[:,main:]
    def row(ref,j,fill):
        r=ref[j:j+1,:]
        return r
    for jp in range(rows//2):
        for h in range(2):
            j=2*jp+h
            pr=pairs_ref[j:j+1,:]; tr=tg_ref[j:j+1,:]; sr=sg_ref[j:j+1,:].astype(F32)
            op=jnp.where(lax.broadcasted_iota(jnp.int32,(n_pairs,exc),0)==pr,1.0,0.0).astype(BF)
            tt=jnp.where(lax.broadcasted_iota(jnp.int32,(na,exc),0)==tr,sr,0.0).astype(BF)
            w=lax.dot_general(op,tt,NT,preferred_element_type=F32).astype(BF)
            c=slice(h*na,(h+1)*na)
            s=jp%2
            wcat[s,0:main,c]=w[:main]; wcat[s,main:2*main,c]=w[:main]
            wcat[s,2*main:2*main+rest,c]=w[main:]; wcat[s,2*main+rest:2*main+2*rest,c]=w[main:]
        g=jnp.dot(vcat[...],wcat[jp%2],preferred_element_type=F32)
        for h in range(2):
            j=2*jp+h
            hi,lo=split(g[:,h*na:(h+1)*na])
            g_ref[j,:n_pairs,:na]=hi; g_ref[j,:n_pairs,na:]=lo
            g_ref[j,n_pairs:,:]=jnp.zeros((g_ref.shape[1]-n_pairs,2*na),BF)
def fold(pairs,tg,sg,v,total_rows):
    rows_here,exc=pairs.shape; n_pairs=v.shape[0]; w=(n_pairs+127)//128*128
    rows=8; ew=(exc+127)//128
    main=n_pairs//128*128; rest=n_pairs-main
    kc=2*n_pairs
    tab=pl.BlockSpec((rows,exc),lambda i:(i,0))
    return pl.pallas_call(functools.partial(fold_kernel,rows),
        out_shape=jax.ShapeDtypeStruct((rows_here,w,2*total_rows),BF),
        grid=(rows_here//rows,),
        in_specs=[tab,tab,tab,pl.BlockSpec((n_pairs,n_pairs),lambda i:(0,0))],
        out_specs=pl.BlockSpec((rows,w,2*total_rows),lambda i:(i,0,0)),
        scratch_shapes=[pltpu.VMEM((n_pairs,kc),BF),pltpu.VMEM((2,kc,2*total_rows),BF),
           pltpu.VMEM((ew,rows_here,128),jnp.int32),pltpu.VMEM((ew,rows_here,128),jnp.int32),pltpu.VMEM((ew,rows_here,128),F32)],
    )(pairs,tg,sg,v)
def gath(x,idx): return jnp.take_along_axis(x,idx,axis=1,mode="promise_in_bounds")
def inv_kernel(chunks,pairs_ref,inv_ref,scr):
    nb,exc=pairs_ref.shape
    last=inv_ref.shape[1]
    ew=(exc+128)//128*128
    def body(g,_):
        b0=pl.multiple_of(g*8,8)
        pr8=pairs_ref[pl.ds(b0,8),:]
        for h in range(4):
            os_=[];xs=[]
            for j in (2*h,2*h+1):
                pr=pr8[j:j+1,:]
                lane=pr&127; ch=pr>>7
                os_.append(jnp.where(lax.broadcasted_iota(I32,(128,exc),0)==lane,1.0,0.0).astype(BF))
                code=(lax.broadcasted_iota(I32,(8,exc),1)-(ew-1)).astype(F32)
                xs.append(jnp.where(lax.broadcasted_iota(I32,(8,exc),0)==ch,code,0.0))
            o=jnp.concatenate(os_,0); x=jnp.concatenate(xs,0).astype(BF)
            r=lax.dot_general(x,o,NT,preferred_element_type=F32)
            for q,j in enumerate((2*h,2*h+1)):
                scr[pl.ds(b0+j,8,stride=nb),:]=r[q*8:(q+1)*8,q*128:(q+1)*128]
        return 0
    lax.fori_loop(0,nb//8,body,0)
    for c in range(chunks):
        inv_ref[c]=scr[c*nb:(c+1)*nb,:].astype(I32)+(ew-1)
def inverse(pairs,n_pairs):
    nb,exc=pairs.shape; chunks=(n_pairs+127)//128
    return pl.pallas_call(functools.partial(inv_kernel,chunks),
       out_shape=jax.ShapeDtypeStruct((chunks,nb,128),I32),
       in_specs=[pl.BlockSpec(memory_space=pltpu.VMEM)],out_specs=pl.BlockSpec(memory_space=pltpu.VMEM),
       scratch_shapes=[pltpu.VMEM((8*nb,128),F32)])(pairs)
def tree(parts,masks):
    lvl=0
    while len(parts)>1:
        parts=[jnp.where(masks[lvl],parts[2*i+1],parts[2*i]) for i in range(len(parts)//2)]; lvl+=1
    return parts[0]
def sig_kernel(c_ref,tg_ref,sg_ref,inv_ref,g_hbm,o_ref,tgs,sgs,vals,lift,gv,sem):
    nk,na,lanes=c_ref.shape
    nb,exc=tg_ref.shape
    ew=tgs.shape[1]; chunks=inv_ref.shape[0]; ni=g_hbm.shape[2]//2
    cp=pltpu.make_async_copy(g_hbm,gv,sem); cp.start()
    tgs[:,:exc]=tg_ref[...]; tgs[:,exc:]=jnp.zeros((nb,ew-exc),I32)
    sgs[:,:exc]=sg_ref[...].astype(F32); sgs[:,exc:]=jnp.zeros((nb,ew-exc),F32)
    bits=nk.bit_length()-1
    def gbody(g,_):
        bs=pl.multiple_of(g*8,8)
        for ec in range(ew//128):
            t=tgs[pl.ds(bs,8),ec*128:(ec+1)*128]; s=sgs[pl.ds(bs,8),ec*128:(ec+1)*128]
            lane=t&127; ch=t>>7
            ms=[(ch&(1<<i))!=0 for i in range(bits)]
            def one(a,_):
                v=tree([gath(c_ref[k,pl.ds(a,8,stride=0),:],lane) for k in range(nk)],ms)*s
                vals[a,pl.ds(bs,8),ec*128:(ec+1)*128]=v
                return 0
            lax.fori_loop(0,na,one,0,unroll=True)
        return 0
    lax.fori_loop(0,nb//8,gbody,0)
    def lbody(g,_):
        b0=pl.multiple_of(g*16,16)
        for pc in range(chunks):
            idx=[inv_ref[pc,pl.ds(pl.multiple_of(b0+8*h,8),8),:] for h in range(2)]
            ln=[i&127 for i in idx]
            ms=[[((i>>7)&(1<<q))!=0 for q in range((ew//128-1).bit_length())] for i in idx]
            def one(a,_):
                x=jnp.concatenate([tree([gath(vals[a,pl.ds(pl.multiple_of(b0+8*h,8),8),ec*128:(ec+1)*128],ln[h]) for ec in range(ew//128)],ms[h]) for h in range(2)],0)
                hi,lo=split(x)
                lift[a,pl.ds(b0,16),pc*128:(pc+1)*128]=hi
                lift[a,pl.ds(nb+b0,16),pc*128:(pc+1)*128]=lo
                return 0
            lax.fori_loop(0,na,one,0,unroll=True)
        return 0
    lax.fori_loop(0,nb//16,lbody,0)
    cp.wait()
    def mm(ap,acc):
        for j in range(2):
            acc=acc+jnp.dot(lift[2*ap+j],gv[2*ap+j],preferred_element_type=F32)
        return acc
    acc=lax.fori_loop(0,na//2,mm,jnp.zeros((2*nb,2*ni),F32))
    tot=(acc[:nb,:ni]+acc[nb:,:ni])+(acc[:nb,ni:]+acc[nb:,ni:])
    o_ref[...]=tot.T
def sig(c,tg,sg,inv,g):
    nk,na,lanes=c.shape; nb,exc=tg.shape; chunks=inv.shape[0]; ni=g.shape[2]//2
    ew=(exc+128)//128*128
    vm=pl.BlockSpec(memory_space=pltpu.VMEM)
    return pl.pallas_call(sig_kernel,out_shape=jax.ShapeDtypeStruct((ni,nb),F32),
       in_specs=[vm]*4+[pl.BlockSpec(memory_space=pl.ANY)],out_specs=vm,
       scratch_shapes=[pltpu.VMEM((nb,ew),I32),pltpu.VMEM((nb,ew),F32),pltpu.VMEM((na,nb,ew),F32),
          pltpu.VMEM((na,2*nb,chunks*128),BF),pltpu.VMEM(g.shape,BF),pltpu.SemaphoreType.DMA(())])(c,tg,sg,inv,g)

def local(
    coeff, integrals, beta_pairs, beta_targets, beta_signs, alpha_pairs, alpha_targets, alpha_signs
):
    n_beta = lax.axis_size("beta")
    n_alpha = lax.axis_size("alpha")
    rows, cols = coeff.shape
    n_pairs = integrals.shape[0]
    table = coeff[None]
    step = 1
    while step < n_beta:
        other = lax.ppermute(table, "beta", [(i, i ^ step) for i in range(n_beta)])
        table = jnp.concatenate([table, other], 0)
        step *= 2
    me = lax.axis_index("beta")
    targets = beta_targets ^ (me * cols)
    g = fold(alpha_pairs, alpha_targets, alpha_signs, integrals, rows * n_alpha)
    inv = inverse(beta_pairs, n_pairs)
    partial = sig(table, targets, beta_signs, inv, g)
    parts = partial.reshape(n_alpha, rows, cols)
    mine = lax.axis_index("alpha")
    total = lax.dynamic_index_in_dim(parts, mine, 0, False)
    for k in range(1, n_alpha):
        block = lax.dynamic_index_in_dim(parts, mine ^ k, 0, False)
        total = total + lax.ppermute(block, "alpha", [(i, i ^ k) for i in range(n_alpha)])
    return total


def solution(mesh):
    placed = (
        P("alpha", "beta"),
        P(),
        P("beta", None),
        P("beta", None),
        P("beta", None),
        P("alpha", None),
        P("alpha", None),
        P("alpha", None),
    )
    return jax.shard_map(
        local, mesh=mesh, in_specs=placed, out_specs=P("alpha", "beta"), check_vma=False
    )
```

```python
import functools

import jax
import jax.numpy as jnp
from jax import lax
from jax.experimental import pallas as pl
from jax.experimental.pallas import tpu as pltpu
from jax.sharding import PartitionSpec as P

BF = jnp.bfloat16
F32 = jnp.float32
I32 = jnp.int32
NT = (((1,), (1,)), ((), ()))
BLOCK = 16


def split(x):
    hi = x.astype(BF)
    return hi, (x - hi.astype(F32)).astype(BF)


def fold_kernel(rows,pairs_ref,tg_ref,sg_ref,v_ref,g_ref,vcat,wcat,rows_p,rows_t,rows_s):
    n_pairs=v_ref.shape[0]; na=g_ref.shape[2]//2
    main=n_pairs//128*128; rest=n_pairs-main
    exc=pairs_ref.shape[1]; ew=rows_p.shape[0]*128
    @pl.when(pl.program_id(0)==0)
    def _():
        hi,lo=split(v_ref[...])
        vcat[:,:main]=hi[:,:main]; vcat[:,main:2*main]=lo[:,:main]
        vcat[:,2*main:2*main+rest]=hi[:,main:]; vcat[:,2*main+rest:2*main+2*rest]=lo[:,main:]
    def row(ref,j,fill):
        r=ref[j:j+1,:]
        return r
    for jp in range(rows//2):
        for h in range(2):
            j=2*jp+h
            pr=pairs_ref[j:j+1,:]; tr=tg_ref[j:j+1,:]; sr=sg_ref[j:j+1,:].astype(F32)
            op=jnp.where(lax.broadcasted_iota(jnp.int32,(n_pairs,exc),0)==pr,1.0,0.0).astype(BF)
            tt=jnp.where(lax.broadcasted_iota(jnp.int32,(na,exc),0)==tr,sr,0.0).astype(BF)
            w=lax.dot_general(op,tt,NT,preferred_element_type=F32).astype(BF)
            c=slice(h*na,(h+1)*na)
            s=jp%2
            wcat[s,0:main,c]=w[:main]; wcat[s,main:2*main,c]=w[:main]
            wcat[s,2*main:2*main+rest,c]=w[main:]; wcat[s,2*main+rest:2*main+2*rest,c]=w[main:]
        g=jnp.dot(vcat[...],wcat[jp%2],preferred_element_type=F32)
        for h in range(2):
            j=2*jp+h
            hi,lo=split(g[:,h*na:(h+1)*na])
            g_ref[j,:n_pairs,:na]=hi; g_ref[j,:n_pairs,na:]=lo
            g_ref[j,n_pairs:,:]=jnp.zeros((g_ref.shape[1]-n_pairs,2*na),BF)
def fold(pairs,tg,sg,v,total_rows):
    rows_here,exc=pairs.shape; n_pairs=v.shape[0]; w=(n_pairs+127)//128*128
    rows=8; ew=(exc+127)//128
    main=n_pairs//128*128; rest=n_pairs-main
    kc=2*n_pairs
    tab=pl.BlockSpec((rows,exc),lambda i:(i,0))
    return pl.pallas_call(functools.partial(fold_kernel,rows),
        out_shape=jax.ShapeDtypeStruct((rows_here,w,2*total_rows),BF),
        grid=(rows_here//rows,),
        in_specs=[tab,tab,tab,pl.BlockSpec((n_pairs,n_pairs),lambda i:(0,0))],
        out_specs=pl.BlockSpec((rows,w,2*total_rows),lambda i:(i,0,0)),
        scratch_shapes=[pltpu.VMEM((n_pairs,kc),BF),pltpu.VMEM((2,kc,2*total_rows),BF),
           pltpu.VMEM((ew,rows_here,128),jnp.int32),pltpu.VMEM((ew,rows_here,128),jnp.int32),pltpu.VMEM((ew,rows_here,128),F32)],
    )(pairs,tg,sg,v)
def gath(x,idx): return jnp.take_along_axis(x,idx,axis=1,mode="promise_in_bounds")
def tree(parts,masks):
    lvl=0
    while len(parts)>1:
        parts=[jnp.where(masks[lvl],parts[2*i+1],parts[2*i]) for i in range(len(parts)//2)]; lvl+=1
    return parts[0]
def sig_kernel(parts,place,c_ref,tg_ref,sg_ref,pr_ref,g_hbm,*refs):
    outs=refs[:parts]
    tgs,sgs,prs,lift,perm,turned,gv,accr,sem=refs[parts:]
    nk,na,lanes=c_ref.shape
    exc,nb=tg_ref.shape
    ew=tgs.shape[1]; chunks=lift.shape[0]; ni=g_hbm.shape[1]//2
    cp=pltpu.make_async_copy(g_hbm,gv,sem); cp.start()
    def flip(ref): return jnp.concatenate([ref[...],jnp.zeros((ew-exc,nb),ref.dtype)],0).T
    tgs[...]=flip(tg_ref)^(place[0]*lanes); sgs[...]=flip(sg_ref).astype(F32); prs[...]=flip(pr_ref)
    bits=nk.bit_length()-1
    seg=nb//8; blk=8*(seg+1)+1
    wide=2*128; nc=(chunks*128+wide-1)//wide
    def body(g,_):
        b0=pl.multiple_of(g*BLOCK,BLOCK)
        tg8=tgs[pl.ds(b0,BLOCK),:]; sg8=sgs[pl.ds(b0,BLOCK),:]; pr8=prs[pl.ds(b0,BLOCK),:]
        for j in range(BLOCK):
            cols=[]
            for ec in range(ew//128):
                t=jnp.broadcast_to(tg8[j:j+1,ec*128:(ec+1)*128],(8,128))
                s=jnp.broadcast_to(sg8[j:j+1,ec*128:(ec+1)*128],(8,128))
                lane=t&127; ch=t>>7
                ms=[(ch&(1<<i))!=0 for i in range(bits)]
                cols.append(jnp.concatenate([tree([gath(c_ref[k,ag*8:(ag+1)*8,:],lane) for k in range(nk)],ms)*s for ag in range(na//8)],0))
            x=jnp.concatenate(cols,1)
            hi,lo=split(x)
            x=jnp.concatenate([hi,lo],0)
            p=pr8[j:j+1,:]
            pl_=p&(wide-1); pc=p>>8
            xm=[]
            for c in range(nc):
                m=jnp.where(pc==c,1.0,0.0).astype(BF)
                xm.append(x*m)
            xm=jnp.concatenate(xm,0)
            o=jnp.where(lax.broadcasted_iota(I32,(wide,ew),0).astype(BF)==pl_.astype(BF),jnp.bfloat16(1),jnp.bfloat16(0))
            r=lax.dot_general(xm,o,NT,preferred_element_type=F32)
            bb=b0+j
            row=bb+lax.div(bb,seg)
            for q in range(chunks):
                c,w=divmod(q,2); cs=slice(w*128,(w+1)*128)
                for r0 in range(0,na,8):
                    t0=c*2*na+r0
                    lift.at[q][pl.ds(row+r0*blk,8,stride=blk),:]=r[t0:t0+8,cs]+r[t0+na:t0+na+8,cs]
        return 0
    lax.fori_loop(0,nb//BLOCK,body,0)
    cp.wait()
    per=4
    def mm(ap):
        parts=[]
        for jj in range(per):
            a=per*ap+jj
            parts+=[jnp.concatenate([lift.at[q][pl.ds(a*blk+rr,8,stride=seg+1),:] for rr in range(seg)],0) for q in range(chunks)]
        hi,lo=split(jnp.concatenate(parts,1))
        kw=per*chunks*128
        return jnp.dot(jnp.concatenate([hi,lo],0),gv[pl.ds(pl.multiple_of(ap*kw,kw),kw),:],preferred_element_type=F32)
    accr[...]=mm(0)
    def st(ap,_):
        accr[...]+=mm(ap); return 0
    lax.fori_loop(1,na//per,st,0)
    acc=accr[...]
    tot=(acc[:nb,:ni]+acc[nb:,:ni])+(acc[:nb,ni:]+acc[nb:,ni:])
    for i0 in range(0,ni,128):
        for rr in range(seg):
            perm.at[i0//128][pl.ds(rr,8,stride=seg),:]=tot[rr*8:rr*8+8,i0:i0+128]
        turned[i0:i0+128,:]=perm[i0//128,:nb].T
    rows=outs[0].shape[0]
    for k in range(parts):
        outs[k][...]=turned[pl.ds(pl.multiple_of((place[1]^k)*rows,rows),rows),:]
def sig(place,c,tg,sg,pr,g,parts):
    nk,na,lanes=c.shape; exc,nb=tg.shape; chunks=g.shape[0]//na//128; ni=g.shape[1]//2
    ew=(exc+127)//128*128
    vm=pl.BlockSpec(memory_space=pltpu.VMEM)
    return pl.pallas_call(functools.partial(sig_kernel,parts),
       out_shape=[jax.ShapeDtypeStruct((ni//parts,nb),F32)]*parts,
       in_specs=[pl.BlockSpec(memory_space=pltpu.SMEM)]+[vm]*4+[pl.BlockSpec(memory_space=pl.ANY)],out_specs=[vm]*parts,
       scratch_shapes=[pltpu.VMEM((nb,ew),I32),pltpu.VMEM((nb,ew),F32),pltpu.VMEM((nb,ew),I32),
          pltpu.VMEM((chunks,(na+1)*(8*(nb//8+1)+1),128),F32),pltpu.VMEM((ni//128,nb+nb//8,128),F32),pltpu.VMEM((ni,nb),F32),
          pltpu.VMEM(g.shape,BF),pltpu.VMEM((2*nb,2*ni),F32),pltpu.SemaphoreType.DMA(())])(place,c,tg,sg,pr,g)


def local(
    coeff, integrals, beta_pairs, beta_targets, beta_signs, alpha_pairs, alpha_targets, alpha_signs
):
    n_beta = lax.axis_size("beta")
    n_alpha = lax.axis_size("alpha")
    rows, cols = coeff.shape
    table = coeff[None]
    step = 1
    while step < n_beta:
        other = lax.ppermute(table, "beta", [(i, i ^ step) for i in range(n_beta)])
        table = jnp.concatenate([table, other], 0)
        step *= 2
    place = jnp.stack([lax.axis_index("beta"), lax.axis_index("alpha")]).astype(I32)
    g = fold(alpha_pairs, alpha_targets, alpha_signs, integrals, rows * n_alpha)
    g = g.reshape(-1, g.shape[2])
    parts = sig(place, table, beta_targets.T, beta_signs.T, beta_pairs.T, g, n_alpha)
    total = parts[0]
    for k in range(1, n_alpha):
        total = total + lax.ppermute(parts[k], "alpha", [(i, i ^ k) for i in range(n_alpha)])
    return total


def solution(mesh):
    placed = (
        P("alpha", "beta"),
        P(),
        P("beta", None),
        P("beta", None),
        P("beta", None),
        P("alpha", None),
        P("alpha", None),
        P("alpha", None),
    )
    return jax.shard_map(
        local, mesh=mesh, in_specs=placed, out_specs=P("alpha", "beta"), check_vma=False
    )
```

```python
import functools

import jax
import jax.numpy as jnp
from jax import lax
from jax.experimental import pallas as pl
from jax.experimental.pallas import tpu as pltpu
from jax.sharding import PartitionSpec as P

BF = jnp.bfloat16
F32 = jnp.float32
I32 = jnp.int32
NT = (((1,), (1,)), ((), ()))
BLOCK = 16
PAIRED = 1


def split(x):
    hi = x.astype(BF)
    return hi, (x - hi.astype(F32)).astype(BF)


def fold_kernel(rows,pairs_ref,tg_ref,sg_ref,v_ref,g_ref,vcat,wcat):
    n_pairs=v_ref.shape[0]; na=g_ref.shape[2]//2
    main=n_pairs//128*128; rest=n_pairs-main
    exc=pairs_ref.shape[1]
    @pl.when(pl.program_id(0)==0)
    def _():
        hi,lo=split(v_ref[...])
        vcat[:,:main]=hi[:,:main]; vcat[:,main:2*main]=lo[:,:main]
        vcat[:,2*main:2*main+rest]=hi[:,main:]; vcat[:,2*main+rest:2*main+2*rest]=lo[:,main:]
    def spread(jp):
        for h in range(2):
            j=2*jp+h
            pr=pairs_ref[j:j+1,:]; tr=tg_ref[j:j+1,:].astype(BF); sr=sg_ref[j:j+1,:].astype(BF)
            ops=[]
            for q0 in range(0,n_pairs,256):
                n=min(256,n_pairs-q0)
                ops.append(jnp.where(lax.broadcasted_iota(I32,(n,exc),0).astype(BF)==(pr-q0).astype(BF),jnp.bfloat16(1),jnp.bfloat16(0)))
            op=jnp.concatenate(ops,0)
            tt=jnp.where(lax.broadcasted_iota(I32,(na,exc),0).astype(BF)==tr,sr,jnp.bfloat16(0))
            w=lax.dot_general(op,tt,NT,preferred_element_type=F32).astype(BF)
            c=slice(h*na,(h+1)*na); s=jp%2
            wcat[s,0:main,c]=w[:main]; wcat[s,main:2*main,c]=w[:main]
            wcat[s,2*main:2*main+rest,c]=w[main:]; wcat[s,2*main+rest:2*main+2*rest,c]=w[main:]
    def mix(jp):
        g=jnp.dot(vcat[...],wcat[jp%2],preferred_element_type=F32)
        for h in range(2):
            j=2*jp+h
            hi,lo=split(g[:,h*na:(h+1)*na])
            g_ref[j,:n_pairs,:na]=hi; g_ref[j,:n_pairs,na:]=lo
            g_ref[j,n_pairs:,:]=jnp.zeros((g_ref.shape[1]-n_pairs,2*na),BF)
    n=rows//2
    spread(0)
    for jp in range(n):
        if jp+1<n: spread(jp+1)
        mix(jp)
def fold(pairs,tg,sg,v,total_rows):
    rows_here,exc=pairs.shape; n_pairs=v.shape[0]; w=(n_pairs+127)//128*128
    rows=8
    kc=2*n_pairs
    tab=pl.BlockSpec((rows,exc),lambda i:(i,0))
    return pl.pallas_call(functools.partial(fold_kernel,rows),
        out_shape=jax.ShapeDtypeStruct((rows_here,w,2*total_rows),BF),
        grid=(rows_here//rows,),
        in_specs=[tab,tab,tab,pl.BlockSpec((n_pairs,n_pairs),lambda i:(0,0))],
        out_specs=pl.BlockSpec((rows,w,2*total_rows),lambda i:(i,0,0)),
        scratch_shapes=[pltpu.VMEM((n_pairs,kc),BF),pltpu.VMEM((2,kc,2*total_rows),BF)],
    )(pairs,tg,sg,v)
def gath(x,idx): return jnp.take_along_axis(x,idx,axis=1,mode="promise_in_bounds")
def tree(parts,masks,low=0,bit=None):
    bit=len(masks) if bit is None else bit
    if bit==0: return parts.get(low)
    left=tree(parts,masks,low,bit-1); right=tree(parts,masks,low+(1<<(bit-1)),bit-1)
    if left is None: return right
    return left if right is None else jnp.where(masks[bit-1],right,left)
def sig_kernel(parts,direct,place,c_ref,tg_ref,sg_ref,pr_ref,g_hbm,*refs):
    outs=refs[:parts]
    tgs,sgs,prs,cs_ref,xf,rs,lift,perm,turned,gv,accr,sem=refs[parts:]
    nk,na,lanes=c_ref.shape
    exc,nb=tg_ref.shape
    ew=tgs.shape[1]; chunks=lift.shape[0]; ni=g_hbm.shape[1]//2
    cp=pltpu.make_async_copy(g_hbm,gv,sem); cp.start()
    def flip(ref): return jnp.concatenate([ref[...],jnp.zeros((ew-exc,nb),ref.dtype)],0).T
    tgs[...]=flip(tg_ref) if direct else flip(tg_ref)^(place[0]*lanes); sgs[...]=flip(sg_ref).astype(F32); prs[...]=flip(pr_ref)
    bits=nk.bit_length()-1
    if PAIRED:
        hi,lo=split(jnp.concatenate([c_ref[k] for k in range(2*PAIRED)],1))
        cs_ref[:na]=hi; cs_ref[na:]=lo
    seg=nb//8; blk=8*(seg+1)+1
    wide=2*128; nc=(chunks*128+wide-1)//wide
    def early(g,slot):
        b0=pl.multiple_of(g*BLOCK,BLOCK)
        tg8=tgs[pl.ds(b0,BLOCK),:]; sg8=sgs[pl.ds(b0,BLOCK),:]
        for j in range(BLOCK):
            tb=tg8[j:j+1,:]; sb=sg8[j:j+1,:].astype(BF)
            o2=jnp.concatenate([jnp.where(lax.broadcasted_iota(I32,(256,ew),0).astype(BF)==(tb-256*m).astype(BF),sb,jnp.bfloat16(0)) for m in range(PAIRED)],0)
            rg=jnp.dot(cs_ref[...],o2,preferred_element_type=F32)
            rs[slot,j]=rg[:na]+rg[na:]
            yield
    def gather(g,slot):
        b0=pl.multiple_of(g*BLOCK,BLOCK)
        tg8=tgs[pl.ds(b0,BLOCK),:]; sg8=sgs[pl.ds(b0,BLOCK),:]
        for j in range(BLOCK):
            cols=[]
            for ec in range(ew//128):
                t=jnp.broadcast_to(tg8[j:j+1,ec*128:(ec+1)*128],(8,128))
                s=jnp.broadcast_to(sg8[j:j+1,ec*128:(ec+1)*128],(8,128))
                lane=t&127; ch=t>>7
                ms=[(ch&(1<<i))!=0 for i in range(bits)]
                s=jnp.where(ch<2*PAIRED,0.0,s)
                for ag in range(na//8):
                    v=tree({k:gath(c_ref[k,ag*8:(ag+1)*8,:],lane) for k in range(2*PAIRED,nk)},ms)*s
                    xf[slot,j,ag*8:ag*8+8,ec*128:(ec+1)*128]=v
            yield
    def raise_(g,slot):
        b0=pl.multiple_of(g*BLOCK,BLOCK)
        pr8=prs[pl.ds(b0,BLOCK),:]
        for j in range(BLOCK):
            p=pr8[j:j+1,:]
            pl_=p&(wide-1); pc=p>>8
            x=xf[slot,j]
            if PAIRED: x=x+rs[slot,j]
            hi,lo=split(x)
            x=jnp.concatenate([hi,lo],0)
            xm=jnp.concatenate([x*jnp.where(pc==c,1.0,0.0).astype(BF) for c in range(nc)],0)
            o=jnp.where(lax.broadcasted_iota(I32,(wide,ew),0).astype(BF)==pl_.astype(BF),jnp.bfloat16(1),jnp.bfloat16(0))
            r=lax.dot_general(xm,o,NT,preferred_element_type=F32)
            bb=b0+j
            row=bb+lax.div(bb,seg)
            for q in range(chunks):
                c,w=divmod(q,2); cw=slice(w*128,(w+1)*128)
                for r0 in range(0,na,8):
                    t0=c*2*na+r0
                    lift.at[q][pl.ds(row+r0*blk,8,stride=blk),:]=r[t0:t0+8,cw]+r[t0+na:t0+na+8,cw]
            yield
    def drive(*gens):
        for _ in range(BLOCK):
            for gen in gens: next(gen)
    groups=nb//BLOCK
    def load(g,slot): return ((early(g,slot),) if PAIRED else ())+(gather(g,slot),)
    drive(*load(0,0))
    def body(g,_):
        slot=g&1
        drive(raise_(g,slot),*load(g+1,1-slot))
        return 0
    lax.fori_loop(0,groups-1,body,0)
    drive(raise_(groups-1,(groups-1)&1))
    cp.wait()
    per=4
    def mm(ap):
        parts=[]
        for jj in range(per):
            a=per*ap+jj
            parts+=[jnp.concatenate([lift.at[q][pl.ds(a*blk+rr,8,stride=seg+1),:] for rr in range(seg)],0) for q in range(chunks)]
        hi,lo=split(jnp.concatenate(parts,1))
        kw=per*chunks*128
        return jnp.dot(jnp.concatenate([hi,lo],0),gv[pl.ds(pl.multiple_of(ap*kw,kw),kw),:],preferred_element_type=F32)
    accr[...]=mm(0)
    def st(ap,_):
        accr[...]+=mm(ap); return 0
    lax.fori_loop(1,na//per,st,0)
    acc=accr[...]
    tot=(acc[:nb,:ni]+acc[nb:,:ni])+(acc[:nb,ni:]+acc[nb:,ni:])
    for i0 in range(0,ni,128):
        for rr in range(seg):
            perm.at[i0//128][pl.ds(rr,8,stride=seg),:]=tot[rr*8:rr*8+8,i0:i0+128]
        turned[i0:i0+128,:]=perm[i0//128,:nb].T
    rows=outs[0].shape[0]
    for k in range(parts):
        outs[k][...]=turned[pl.ds(pl.multiple_of((place[1]^k)*rows,rows),rows),:]
def sig(place,c,tg,sg,pr,g,parts,direct):
    nk,na,lanes=c.shape; exc,nb=tg.shape; chunks=g.shape[0]//na//128; ni=g.shape[1]//2
    ew=(exc+127)//128*128
    vm=pl.BlockSpec(memory_space=pltpu.VMEM)
    return pl.pallas_call(functools.partial(sig_kernel,parts,direct),
       out_shape=[jax.ShapeDtypeStruct((ni//parts,nb),F32)]*parts,
       in_specs=[pl.BlockSpec(memory_space=pltpu.SMEM)]+[vm]*4+[pl.BlockSpec(memory_space=pl.ANY)],out_specs=[vm]*parts,
       scratch_shapes=[pltpu.VMEM((nb,ew),I32),pltpu.VMEM((nb,ew),F32),pltpu.VMEM((nb,ew),I32),pltpu.VMEM((2*na,256*max(PAIRED,1)),BF),pltpu.VMEM((2,BLOCK,na,ew),F32),pltpu.VMEM((2,BLOCK,na,ew),F32),
          pltpu.VMEM((chunks,(na+1)*(8*(nb//8+1)+1),128),F32),pltpu.VMEM((ni//128,nb+nb//8,128),F32),pltpu.VMEM((ni,nb),F32),pltpu.VMEM(g.shape,BF),pltpu.VMEM((2*nb,2*ni),F32),pltpu.SemaphoreType.DMA(())])(place,c,tg,sg,pr,g)


def local(
    coeff, integrals, beta_pairs, beta_targets, beta_signs, alpha_pairs, alpha_targets, alpha_signs
):
    n_beta = lax.axis_size("beta")
    n_alpha = lax.axis_size("alpha")
    rows, cols = coeff.shape
    table = jnp.broadcast_to(coeff[None], (n_beta, rows, cols))
    table = lax.all_to_all(table, "beta", 0, 0)
    place = jnp.stack([lax.axis_index("beta"), lax.axis_index("alpha")]).astype(I32)
    g = fold(alpha_pairs, alpha_targets, alpha_signs, integrals, rows * n_alpha)
    g = g.reshape(-1, g.shape[2])
    parts = sig(place, table, beta_targets.T, beta_signs.T, beta_pairs.T, g, n_alpha, True)
    total = parts[0]
    for k in range(1, n_alpha):
        total = total + lax.ppermute(parts[k], "alpha", [(i, i ^ k) for i in range(n_alpha)])
    return total


def solution(mesh):
    placed = (
        P("alpha", "beta"),
        P(),
        P("beta", None),
        P("beta", None),
        P("beta", None),
        P("alpha", None),
        P("alpha", None),
        P("alpha", None),
    )
    return jax.shard_map(
        local, mesh=mesh, in_specs=placed, out_specs=P("alpha", "beta"), check_vma=False
    )
```

```python
import functools

import jax
import jax.numpy as jnp
from jax import lax
from jax.experimental import pallas as pl
from jax.experimental.pallas import tpu as pltpu
from jax.sharding import PartitionSpec as P

BF = jnp.bfloat16
F32 = jnp.float32
I32 = jnp.int32
NT = (((1,), (1,)), ((), ()))
BLOCK = 16
PAIRED = 1
GRANT_P = 30 * 2**20
GRANT_A = 30 * 2**20
GRANT_B = 30 * 2**20


def split(x):
    hi = x.astype(BF)
    return hi, (x - hi.astype(F32)).astype(BF)


def prepare_kernel(v_hbm, pairs_hbm, tg_hbm, sg_hbm, vcat, tabs, v_v, sems):
    pieces = ((v_hbm, v_v), (pairs_hbm, tabs.at[0]), (tg_hbm, tabs.at[1]), (sg_hbm, tabs.at[2]))
    copies = [pltpu.make_async_copy(src, dst, sems.at[k]) for k, (src, dst) in enumerate(pieces)]
    for copy in copies:
        copy.start()
    for copy in copies:
        copy.wait()
    n_pairs = v_v.shape[0]
    main = n_pairs // 128 * 128
    rest = n_pairs - main
    hi, lo = split(v_v[...])
    vcat[:, :main] = hi[:, :main]
    vcat[:, main : 2 * main] = lo[:, :main]
    if rest:
        vcat[:, 2 * main : 2 * main + rest] = hi[:, main:]
        vcat[:, 2 * main + rest : 2 * main + 2 * rest] = lo[:, main:]


def prepare(*args):
    v, pairs = args[:2]
    vm = pl.BlockSpec(memory_space=pltpu.VMEM)
    hbm = pl.BlockSpec(memory_space=pltpu.MemorySpace.HBM)
    args = [pltpu.with_memory_space_constraint(x, pltpu.MemorySpace.HBM) for x in args]
    return pl.pallas_call(
        prepare_kernel,
        out_shape=[
            jax.ShapeDtypeStruct((v.shape[0], 2 * v.shape[0]), BF),
            jax.ShapeDtypeStruct((3,) + pairs.shape, I32),
        ],
        in_specs=[hbm] * 4,
        out_specs=[vm] * 2,
        scratch_shapes=[pltpu.VMEM(v.shape, F32), pltpu.SemaphoreType.DMA((4,))],
        compiler_params=pltpu.CompilerParams(vmem_limit_bytes=GRANT_P),
        cost_estimate=pl.CostEstimate(flops=10**6, bytes_accessed=3 * 10**6, transcendentals=0),
    )(*args)


def fold_kernel(vcat, tabs, g_ref, wcat):
    n_pairs = vcat.shape[0]
    na = g_ref.shape[1] // 2
    _, rows, _ = tabs.shape
    width = g_ref.shape[0] // rows
    main = n_pairs // 128 * 128
    rest = n_pairs - main

    def group(g, _):
        a0 = pl.multiple_of(g * 8, 8)
        pairs8, tg8, sg8 = (tabs[k, pl.ds(a0, 8), :] for k in range(3))

        def spread(jp):
            for h in range(2):
                j = 2 * jp + h
                op = one_hot(pairs8[j : j + 1, :], n_pairs, None)
                tt = one_hot(tg8[j : j + 1, :], na, sg8[j : j + 1, :].astype(BF))
                w = lax.dot_general(op, tt, NT, preferred_element_type=F32).astype(BF)
                c = slice(h * na, (h + 1) * na)
                s = jp % 2
                wcat[s, 0:main, c] = w[:main]
                wcat[s, main : 2 * main, c] = w[:main]
                if rest:
                    wcat[s, 2 * main : 2 * main + rest, c] = w[main:]
                    wcat[s, 2 * main + rest : 2 * main + 2 * rest, c] = w[main:]

        def mix(jp):
            g2 = jnp.dot(vcat[...], wcat[jp % 2], preferred_element_type=F32)
            for h in range(2):
                a = a0 + 2 * jp + h
                hi, lo = split(g2[:, h * na : (h + 1) * na])
                at = pl.multiple_of(a * width, 128)
                g_ref[pl.ds(at, n_pairs), :na] = hi
                g_ref[pl.ds(at, n_pairs), na:] = lo
                g_ref[pl.ds(pl.multiple_of(at + n_pairs, 16), width - n_pairs), :] = jnp.zeros((width - n_pairs, 2 * na), BF)

        spread(0)
        for jp in range(4):
            if jp < 3:
                spread(jp + 1)
            mix(jp)
        return 0

    lax.fori_loop(0, rows // 8, group, 0)


def one_hot(row, size, value):
    one = jnp.bfloat16(1) if value is None else value
    parts = []
    for start in range(0, size, 256):
        n = min(256, size - start)
        ids = lax.broadcasted_iota(I32, (n, row.shape[1]), 0).astype(BF)
        parts.append(jnp.where(ids == (row - start).astype(BF), one, jnp.bfloat16(0)))
    return jnp.concatenate(parts, 0)


def fold(vcat, tabs, total_rows):
    n_pairs = vcat.shape[0]
    width = (n_pairs + 127) // 128 * 128
    vm = pl.BlockSpec(memory_space=pltpu.VMEM)
    return pl.pallas_call(
        fold_kernel,
        out_shape=jax.ShapeDtypeStruct((tabs.shape[1] * width, 2 * total_rows), BF),
        in_specs=[vm] * 2,
        out_specs=vm,
        scratch_shapes=[pltpu.VMEM((2, 2 * n_pairs, 2 * total_rows), BF)],
        compiler_params=pltpu.CompilerParams(vmem_limit_bytes=GRANT_A),
        cost_estimate=pl.CostEstimate(flops=10 * 10**9, bytes_accessed=12 * 10**6, transcendentals=0),
    )(vcat, tabs)


def gath(x,idx): return jnp.take_along_axis(x,idx,axis=1,mode="promise_in_bounds")


def tree(parts,masks,low=0,bit=None):
    bit=len(masks) if bit is None else bit
    if bit==0: return parts.get(low)
    left=tree(parts,masks,low,bit-1); right=tree(parts,masks,low+(1<<(bit-1)),bit-1)
    if left is None: return right
    return left if right is None else jnp.where(masks[bit-1],right,left)


def sig_kernel(parts,count,*args):
    c_refs=args[:count]
    tg_ref,sg_ref,pr_ref,gv,*refs=args[count:]
    outs=refs[:parts]
    tgs,sgs,prs,cs_ref,xf,rs,lift,perm,turned,accr=refs[parts:]
    per_ref,na,lanes=c_refs[0].shape; nk=count*per_ref
    def chunk(k): return c_refs[k//per_ref].at[k%per_ref]
    exc,nb=tg_ref.shape
    ew=tgs.shape[1]; chunks=lift.shape[0]; ni=gv.shape[1]//2
    def flip(ref): return jnp.concatenate([ref[...],jnp.zeros((ew-exc,nb),ref.dtype)],0).T
    tgs[...]=flip(tg_ref)^(lax.axis_index("beta")*lanes); sgs[...]=flip(sg_ref).astype(F32); prs[...]=flip(pr_ref)
    bits=nk.bit_length()-1
    if PAIRED:
        hi,lo=split(jnp.concatenate([chunk(k)[...] for k in range(2*PAIRED)],1))
        cs_ref[:na]=hi; cs_ref[na:]=lo
    seg=nb//8; blk=8*(seg+1)+1
    wide=2*128; nc=(chunks*128+wide-1)//wide
    def early(g,slot):
        b0=pl.multiple_of(g*BLOCK,BLOCK)
        tg8=tgs[pl.ds(b0,BLOCK),:]; sg8=sgs[pl.ds(b0,BLOCK),:]
        for j in range(BLOCK):
            tb=tg8[j:j+1,:]; sb=sg8[j:j+1,:].astype(BF)
            o2=jnp.concatenate([jnp.where(lax.broadcasted_iota(I32,(256,ew),0).astype(BF)==(tb-256*m).astype(BF),sb,jnp.bfloat16(0)) for m in range(PAIRED)],0)
            rg=jnp.dot(cs_ref[...],o2,preferred_element_type=F32)
            rs[slot,j]=rg[:na]+rg[na:]
            yield
    def gather(g,slot):
        b0=pl.multiple_of(g*BLOCK,BLOCK)
        tg8=tgs[pl.ds(b0,BLOCK),:]; sg8=sgs[pl.ds(b0,BLOCK),:]
        for j in range(BLOCK):
            for ec in range(ew//128):
                t=jnp.broadcast_to(tg8[j:j+1,ec*128:(ec+1)*128],(8,128))
                s=jnp.broadcast_to(sg8[j:j+1,ec*128:(ec+1)*128],(8,128))
                lane=t&127; ch=t>>7
                ms=[(ch&(1<<i))!=0 for i in range(bits)]
                s=jnp.where(ch<2*PAIRED,0.0,s)
                for ag in range(na//8):
                    v=tree({k:gath(chunk(k)[ag*8:(ag+1)*8,:],lane) for k in range(2*PAIRED,nk)},ms)*s
                    xf[slot,j,ag*8:ag*8+8,ec*128:(ec+1)*128]=v
            yield
    def raise_(g,slot):
        b0=pl.multiple_of(g*BLOCK,BLOCK)
        pr8=prs[pl.ds(b0,BLOCK),:]
        for j in range(BLOCK):
            p=pr8[j:j+1,:]
            pl_=p&(wide-1); pc=p>>8
            x=xf[slot,j]
            if PAIRED: x=x+rs[slot,j]
            hi,lo=split(x)
            x=jnp.concatenate([hi,lo],0)
            xm=jnp.concatenate([x*jnp.where(pc==c,1.0,0.0).astype(BF) for c in range(nc)],0)
            o=jnp.where(lax.broadcasted_iota(I32,(wide,ew),0).astype(BF)==pl_.astype(BF),jnp.bfloat16(1),jnp.bfloat16(0))
            r=lax.dot_general(xm,o,NT,preferred_element_type=F32)
            bb=b0+j
            row=bb+lax.div(bb,seg)
            for q in range(chunks):
                c,w=divmod(q,2); cw=slice(w*128,(w+1)*128)
                for r0 in range(0,na,8):
                    t0=c*2*na+r0
                    lift.at[q][pl.ds(row+r0*blk,8,stride=blk),:]=r[t0:t0+8,cw]+r[t0+na:t0+na+8,cw]
            yield
    def drive(*gens):
        for _ in range(BLOCK):
            for gen in gens: next(gen)
    groups=nb//BLOCK
    def load(g,slot): return ((early(g,slot),) if PAIRED else ())+(gather(g,slot),)
    drive(*load(0,0))
    def body(g,_):
        slot=g&1
        drive(raise_(g,slot),*load(g+1,1-slot))
        return 0
    lax.fori_loop(0,groups-1,body,0)
    drive(raise_(groups-1,(groups-1)&1))
    per=4
    def mm(ap):
        parts=[]
        for jj in range(per):
            a=per*ap+jj
            parts+=[jnp.concatenate([lift.at[q][pl.ds(a*blk+rr,8,stride=seg+1),:] for rr in range(seg)],0) for q in range(chunks)]
        hi,lo=split(jnp.concatenate(parts,1))
        kw=per*chunks*128
        return jnp.dot(jnp.concatenate([hi,lo],0),gv[pl.ds(pl.multiple_of(ap*kw,kw),kw),:],preferred_element_type=F32)
    accr[...]=mm(0)
    def st(ap,_):
        accr[...]+=mm(ap); return 0
    lax.fori_loop(1,na//per,st,0)
    acc=accr[...]
    tot=(acc[:nb,:ni]+acc[nb:,:ni])+(acc[:nb,ni:]+acc[nb:,ni:])
    for i0 in range(0,ni,128):
        for rr in range(seg):
            perm.at[i0//128][pl.ds(rr,8,stride=seg),:]=tot[rr*8:rr*8+8,i0:i0+128]
        turned[i0:i0+128,:]=perm[i0//128,:nb].T
    rows=outs[0].shape[0]
    for k in range(parts):
        outs[k][...]=turned[pl.ds(pl.multiple_of((lax.axis_index("alpha")^k)*rows,rows),rows),:]


def sig(c,tg,sg,pr,g,parts):
    _,na,_=c[0].shape; exc,nb=tg.shape; chunks=g.shape[0]//na//128; ni=g.shape[1]//2
    ew=(exc+127)//128*128
    vm=pl.BlockSpec(memory_space=pltpu.VMEM)
    return pl.pallas_call(functools.partial(sig_kernel,parts,len(c)),
       out_shape=[jax.ShapeDtypeStruct((ni//parts,nb),F32)]*parts,
       in_specs=[vm]*(4+len(c)),out_specs=[vm]*parts,
       scratch_shapes=[pltpu.VMEM((nb,ew),I32),pltpu.VMEM((nb,ew),F32),pltpu.VMEM((nb,ew),I32),pltpu.VMEM((2*na,256*max(PAIRED,1)),BF),pltpu.VMEM((2,BLOCK,na,ew),F32),pltpu.VMEM((2,BLOCK,na,ew),F32),
          pltpu.VMEM((chunks,(na+1)*(8*(nb//8+1)+1),128),F32),pltpu.VMEM((ni//128,nb+nb//8,128),F32),pltpu.VMEM((ni,nb),F32),pltpu.VMEM((2*nb,2*ni),F32)],
       compiler_params=pltpu.CompilerParams(vmem_limit_bytes=GRANT_B))(*c,tg,sg,pr,g)


def local(
    coeff, integrals, beta_pairs, beta_targets, beta_signs, alpha_pairs, alpha_targets, alpha_signs
):
    n_beta = lax.axis_size("beta")
    n_alpha = lax.axis_size("alpha")
    rows, _ = coeff.shape
    other = lax.ppermute(coeff, "beta", [(i, i ^ 1) for i in range(n_beta)])
    vcat, tabs = prepare(integrals, alpha_pairs, alpha_targets, alpha_signs)
    tables = [jnp.stack([coeff, other])]
    for k in range(2, n_beta, 2):
        tables.append(lax.ppermute(tables[0], "beta", [(i, i ^ k) for i in range(n_beta)]))
    g = fold(vcat, tabs, rows * n_alpha)
    parts = sig(tables, beta_targets.T, beta_signs.T, beta_pairs.T, g, n_alpha)
    total = parts[0]
    for k in range(1, n_alpha):
        total = total + lax.ppermute(parts[k], "alpha", [(i, i ^ k) for i in range(n_alpha)])
    return total


def solution(mesh):
    placed = (
        P("alpha", "beta"),
        P(),
        P("beta", None),
        P("beta", None),
        P("beta", None),
        P("alpha", None),
        P("alpha", None),
        P("alpha", None),
    )

    return jax.shard_map(local, mesh=mesh, in_specs=placed, out_specs=P("alpha", "beta"), check_vma=False)
```

```python
import functools

import jax
import jax.numpy as jnp
from jax import lax
from jax.experimental import pallas as pl
from jax.experimental.pallas import tpu as pltpu
from jax.sharding import PartitionSpec as P

BF = jnp.bfloat16
F32 = jnp.float32
I32 = jnp.int32
NT = (((1,), (1,)), ((), ()))
BLOCK = 16
PAIRED = 1
GRANT_P = 30 * 2**20
GRANT_A = 30 * 2**20
GRANT_B = 30 * 2**20


def split(x):
    hi = x.astype(BF)
    return hi, (x - hi.astype(F32)).astype(BF)


def prepare_kernel(v_hbm, pairs_hbm, tg_hbm, sg_hbm, vcat, tabs, v_v, sems):
    pieces = ((v_hbm, v_v), (pairs_hbm, tabs.at[0]), (tg_hbm, tabs.at[1]), (sg_hbm, tabs.at[2]))
    copies = [pltpu.make_async_copy(src, dst, sems.at[k]) for k, (src, dst) in enumerate(pieces)]
    for copy in copies:
        copy.start()
    for copy in copies:
        copy.wait()
    n_pairs = v_v.shape[0]
    main = n_pairs // 128 * 128
    rest = n_pairs - main
    hi, lo = split(v_v[...])
    vcat[:, :main] = hi[:, :main]
    vcat[:, main : 2 * main] = lo[:, :main]
    if rest:
        vcat[:, 2 * main : 2 * main + rest] = hi[:, main:]
        vcat[:, 2 * main + rest : 2 * main + 2 * rest] = lo[:, main:]


def prepare(*args):
    v, pairs = args[:2]
    vm = pl.BlockSpec(memory_space=pltpu.VMEM)
    hbm = pl.BlockSpec(memory_space=pltpu.MemorySpace.HBM)
    args = [pltpu.with_memory_space_constraint(x, pltpu.MemorySpace.HBM) for x in args]
    return pl.pallas_call(
        prepare_kernel,
        out_shape=[
            jax.ShapeDtypeStruct((v.shape[0], 2 * v.shape[0]), BF),
            jax.ShapeDtypeStruct((3,) + pairs.shape, I32),
        ],
        in_specs=[hbm] * 4,
        out_specs=[vm] * 2,
        scratch_shapes=[pltpu.VMEM(v.shape, F32), pltpu.SemaphoreType.DMA((4,))],
        compiler_params=pltpu.CompilerParams(vmem_limit_bytes=GRANT_P),
        cost_estimate=pl.CostEstimate(flops=10**6, bytes_accessed=3 * 10**6, transcendentals=0),
    )(*args)


def fold_kernel(vcat, tabs, g_ref, wcat):
    n_pairs = vcat.shape[0]
    na = g_ref.shape[1] // 2
    _, rows, _ = tabs.shape
    width = g_ref.shape[0] // rows
    main = n_pairs // 128 * 128
    rest = n_pairs - main

    def group(g, _):
        a0 = pl.multiple_of(g * 8, 8)
        pairs8, tg8, sg8 = (tabs[k, pl.ds(a0, 8), :] for k in range(3))

        def spread(jp, hs=(0, 1)):
            for h in hs:
                j = 2 * jp + h
                op = one_hot(pairs8[j : j + 1, :], n_pairs, None)
                tt = one_hot(tg8[j : j + 1, :], na, sg8[j : j + 1, :].astype(BF))
                w = lax.dot_general(op, tt, NT, preferred_element_type=F32).astype(BF)
                c = slice(h * na, (h + 1) * na)
                s = jp % 3
                wcat[s, 0:main, c] = w[:main]
                wcat[s, main : 2 * main, c] = w[:main]
                if rest:
                    wcat[s, 2 * main : 2 * main + rest, c] = w[main:]
                    wcat[s, 2 * main + rest : 2 * main + 2 * rest, c] = w[main:]

        def mix(jp):
            g2 = jnp.dot(vcat[...], wcat[jp % 3], preferred_element_type=F32)
            for h in range(2):
                a = a0 + 2 * jp + h
                hi, lo = split(g2[:, h * na : (h + 1) * na])
                at = pl.multiple_of(a * width, 128)
                g_ref[pl.ds(at, n_pairs), :na] = hi
                g_ref[pl.ds(at, n_pairs), na:] = lo
                g_ref[pl.ds(pl.multiple_of(at + n_pairs, 16), width - n_pairs), :] = jnp.zeros((width - n_pairs, 2 * na), BF)

        spread(0)
        spread(1)
        for jp in range(4):
            mix(jp)
            if jp < 2:
                spread(jp + 2)
        return 0

    lax.fori_loop(0, rows // 8, group, 0)


def one_hot(row, size, value):
    one = jnp.bfloat16(1) if value is None else value
    parts = []
    for start in range(0, size, 256):
        n = min(256, size - start)
        ids = lax.broadcasted_iota(I32, (n, row.shape[1]), 0).astype(BF)
        parts.append(jnp.where(ids == (row - start).astype(BF), one, jnp.bfloat16(0)))
    return jnp.concatenate(parts, 0)


def fold(vcat, tabs, total_rows):
    n_pairs = vcat.shape[0]
    width = (n_pairs + 127) // 128 * 128
    vm = pl.BlockSpec(memory_space=pltpu.VMEM)
    return pl.pallas_call(
        fold_kernel,
        out_shape=jax.ShapeDtypeStruct((tabs.shape[1] * width, 2 * total_rows), BF),
        in_specs=[vm] * 2,
        out_specs=vm,
        scratch_shapes=[pltpu.VMEM((3, 2 * n_pairs, 2 * total_rows), BF)],
        compiler_params=pltpu.CompilerParams(vmem_limit_bytes=GRANT_A),
        cost_estimate=pl.CostEstimate(flops=10 * 10**9, bytes_accessed=12 * 10**6, transcendentals=0),
    )(vcat, tabs)


def gath(x,idx): return jnp.take_along_axis(x,idx,axis=1,mode="promise_in_bounds")


def tree(parts,masks,low=0,bit=None):
    bit=len(masks) if bit is None else bit
    if bit==0: return parts.get(low)
    left=tree(parts,masks,low,bit-1); right=tree(parts,masks,low+(1<<(bit-1)),bit-1)
    if left is None: return right
    return left if right is None else jnp.where(masks[bit-1],right,left)


def sig_kernel(parts,count,*args):
    c_refs=args[:count]
    tg_ref,sg_ref,pr_ref,gv,*refs=args[count:]
    outs=refs[:parts]
    tgs,sgs,prs,cs_ref,xf,rs,lift,perm,turned,accr=refs[parts:]
    per_ref,na,lanes=c_refs[0].shape; nk=count*per_ref
    def chunk(k): return c_refs[k//per_ref].at[k%per_ref]
    exc,nb=tg_ref.shape
    ew=tgs.shape[1]; chunks=lift.shape[0]; ni=gv.shape[1]//2
    def flip(ref): return jnp.concatenate([ref[...],jnp.zeros((ew-exc,nb),ref.dtype)],0).T
    tgs[...]=flip(tg_ref)^(lax.axis_index("beta")*lanes); sgs[...]=flip(sg_ref).astype(F32); prs[...]=flip(pr_ref)
    bits=nk.bit_length()-1
    if PAIRED:
        hi,lo=split(jnp.concatenate([chunk(k)[...] for k in range(2*PAIRED)],1))
        cs_ref[:na]=hi; cs_ref[na:]=lo
    seg=nb//8; blk=8*(seg+1)+1
    wide=2*128; nc=(chunks*128+wide-1)//wide
    def early(g,slot):
        b0=pl.multiple_of(g*BLOCK,BLOCK)
        tg8=tgs[pl.ds(b0,BLOCK),:]; sg8=sgs[pl.ds(b0,BLOCK),:]
        for j in range(BLOCK):
            tb=tg8[j:j+1,:]; sb=sg8[j:j+1,:].astype(BF)
            o2=jnp.concatenate([jnp.where(lax.broadcasted_iota(I32,(256,ew),0).astype(BF)==(tb-256*m).astype(BF),sb,jnp.bfloat16(0)) for m in range(PAIRED)],0)
            rg=jnp.dot(cs_ref[...],o2,preferred_element_type=F32)
            rs[slot,j]=rg[:na]+rg[na:]
            yield
    def gather(g,slot):
        b0=pl.multiple_of(g*BLOCK,BLOCK)
        tg8=tgs[pl.ds(b0,BLOCK),:]; sg8=sgs[pl.ds(b0,BLOCK),:]
        for j in range(BLOCK):
            for ec in range(ew//128):
                t=jnp.broadcast_to(tg8[j:j+1,ec*128:(ec+1)*128],(8,128))
                s=jnp.broadcast_to(sg8[j:j+1,ec*128:(ec+1)*128],(8,128))
                lane=t&127; ch=t>>7
                ms=[(ch&(1<<i))!=0 for i in range(bits)]
                s=jnp.where(ch<2*PAIRED,0.0,s)
                for ag in range(na//8):
                    v=tree({k:gath(chunk(k)[ag*8:(ag+1)*8,:],lane) for k in range(2*PAIRED,nk)},ms)*s
                    xf[slot,j,ag*8:ag*8+8,ec*128:(ec+1)*128]=v
            yield
    def raise_(g,slot):
        b0=pl.multiple_of(g*BLOCK,BLOCK)
        pr8=prs[pl.ds(b0,BLOCK),:]
        for j in range(BLOCK):
            p=pr8[j:j+1,:]
            pl_=p&(wide-1); pc=p>>8
            x=xf[slot,j]
            if PAIRED: x=x+rs[slot,j]
            hi,lo=split(x)
            x=jnp.concatenate([hi,lo],0)
            xm=jnp.concatenate([x*jnp.where(pc==c,1.0,0.0).astype(BF) for c in range(nc)],0)
            o=jnp.where(lax.broadcasted_iota(I32,(wide,ew),0).astype(BF)==pl_.astype(BF),jnp.bfloat16(1),jnp.bfloat16(0))
            r=lax.dot_general(xm,o,NT,preferred_element_type=F32)
            bb=b0+j
            row=bb+lax.div(bb,seg)
            for q in range(chunks):
                c,w=divmod(q,2); cw=slice(w*128,(w+1)*128)
                for r0 in range(0,na,8):
                    t0=c*2*na+r0
                    lift.at[q][pl.ds(row+r0*blk,8,stride=blk),:]=r[t0:t0+8,cw]+r[t0+na:t0+na+8,cw]
            yield
    def drive(*gens):
        for _ in range(BLOCK):
            for gen in gens: next(gen)
    groups=nb//BLOCK
    def load(g,slot): return ((early(g,slot),) if PAIRED else ())+(gather(g,slot),)
    drive(*load(0,0))
    def body(g,_):
        slot=g&1
        drive(raise_(g,slot),*load(g+1,1-slot))
        return 0
    lax.fori_loop(0,groups-1,body,0)
    drive(raise_(groups-1,(groups-1)&1))
    per=8
    def mm(ap):
        parts=[]
        for jj in range(per):
            a=per*ap+jj
            parts+=[jnp.concatenate([lift.at[q][pl.ds(a*blk+rr,8,stride=seg+1),:] for rr in range(seg)],0) for q in range(chunks)]
        hi,lo=split(jnp.concatenate(parts,1))
        kw=per*chunks*128
        return jnp.dot(jnp.concatenate([hi,lo],0),gv[pl.ds(pl.multiple_of(ap*kw,kw),kw),:],preferred_element_type=F32)
    accr[...]=mm(0)
    def st(ap,_):
        accr[...]+=mm(ap); return 0
    lax.fori_loop(1,na//per,st,0)
    acc=accr[...]
    tot=(acc[:nb,:ni]+acc[nb:,:ni])+(acc[:nb,ni:]+acc[nb:,ni:])
    for i0 in range(0,ni,128):
        for rr in range(seg):
            perm.at[i0//128][pl.ds(rr,8,stride=seg),:]=tot[rr*8:rr*8+8,i0:i0+128]
        turned[i0:i0+128,:]=perm[i0//128,:nb].T
    rows=outs[0].shape[0]
    for k in range(parts):
        outs[k][...]=turned[pl.ds(pl.multiple_of((lax.axis_index("alpha")^k)*rows,rows),rows),:]


def sig(c,tg,sg,pr,g,parts):
    _,na,_=c[0].shape; exc,nb=tg.shape; chunks=g.shape[0]//na//128; ni=g.shape[1]//2
    ew=(exc+127)//128*128
    vm=pl.BlockSpec(memory_space=pltpu.VMEM)
    return pl.pallas_call(functools.partial(sig_kernel,parts,len(c)),
       out_shape=[jax.ShapeDtypeStruct((ni//parts,nb),F32)]*parts,
       in_specs=[vm]*(4+len(c)),out_specs=[vm]*parts,
       scratch_shapes=[pltpu.VMEM((nb,ew),I32),pltpu.VMEM((nb,ew),F32),pltpu.VMEM((nb,ew),I32),pltpu.VMEM((2*na,256*max(PAIRED,1)),BF),pltpu.VMEM((2,BLOCK,na,ew),F32),pltpu.VMEM((2,BLOCK,na,ew),F32),
          pltpu.VMEM((chunks,(na+1)*(8*(nb//8+1)+1),128),F32),pltpu.VMEM((ni//128,nb+nb//8,128),F32),pltpu.VMEM((ni,nb),F32),pltpu.VMEM((2*nb,2*ni),F32)],
       compiler_params=pltpu.CompilerParams(vmem_limit_bytes=GRANT_B))(*c,tg,sg,pr,g)


def local(
    coeff, integrals, beta_pairs, beta_targets, beta_signs, alpha_pairs, alpha_targets, alpha_signs
):
    n_beta = lax.axis_size("beta")
    n_alpha = lax.axis_size("alpha")
    rows, _ = coeff.shape
    other = lax.ppermute(coeff, "beta", [(i, i ^ 1) for i in range(n_beta)])
    vcat, tabs = prepare(integrals, alpha_pairs, alpha_targets, alpha_signs)
    tables = [jnp.stack([coeff, other])]
    for k in range(2, n_beta, 2):
        tables.append(lax.ppermute(tables[0], "beta", [(i, i ^ k) for i in range(n_beta)]))
    g = fold(vcat, tabs, rows * n_alpha)
    parts = sig(tables, beta_targets.T, beta_signs.T, beta_pairs.T, g, n_alpha)
    total = parts[0]
    for k in range(1, n_alpha):
        total = total + lax.ppermute(parts[k], "alpha", [(i, i ^ k) for i in range(n_alpha)])
    return total


def solution(mesh):
    placed = (
        P("alpha", "beta"),
        P(),
        P("beta", None),
        P("beta", None),
        P("beta", None),
        P("alpha", None),
        P("alpha", None),
        P("alpha", None),
    )

    return jax.shard_map(local, mesh=mesh, in_specs=placed, out_specs=P("alpha", "beta"), check_vma=False)
```
